128 devices in a mesh: seq: 16 (over y_lo, z, core), tensor: 8 (over x, y_hi).
Axes of the slice: x: 4, y: 4 (y_hi: 2, y_lo: 2; y = y_hi * 2 + y_lo), z: 4, core: 2. Of those that a mesh axis runs over, the one named last changes fastest.
Arguments:
- activations: bfloat16 [1024, 131072], P('tensor', 'seq'), may hold values from -24 to 24
- first_factor: bfloat16 [512, 512], replicated, may hold values from -0.25 to 0.25
- spectral: float32 [1024, 131072], P('tensor', 'seq'), may hold values from -4 to 4
- second_factor: float32 [256, 256], replicated, may hold values from -0.375 to 0.375
- gate_scale: float32 [1024], replicated, may hold values from -4 to 4
- gate_shift: float32 [1024], replicated, may hold values from -4 to 4
- expand_weight: bfloat16 [1024, 6144], P(None, ('seq', 'tensor')), may hold values from -0.1875 to 0.1875
- reduce_weight: bfloat16 [6144, 1024], P(('seq', 'tensor')), may hold values from -0.3125 to 0.3125
Outputs:
- layer_out: bfloat16 [1024, 131072], P('tensor', 'seq')
The draws below stay inside these ranges and needn't reach their ends.
All inputs are finite; a program needn't handle non-finite values.
Results may differ from the reference program's by a relative error of at most 0.0052.
Values may be sent and summed in bfloat16 or wider, within the bound.
A program may use at most 128 MiB of HBM per device.

```python
import math
import jax
import jax.numpy as jnp
from jax import lax

A = 256
B = 512
C = 1024
H = 6144
TOKENS = 131072
DEVICES = 128


def draw_activations(key, part):
    key_chan, key_base, key_rows = jax.random.split(key, 3)
    channel_scale = jnp.exp(jax.random.uniform(key_chan, (C, 1), jnp.float32, math.log(0.3), math.log(3.0)))
    row_scale = jnp.exp(jax.random.uniform(key_rows, (1, A * B), jnp.float32, math.log(0.5), math.log(2.0)))
    base = jax.random.truncated_normal(key_base, -4.0, 4.0, (C, A * B), jnp.float32)
    return (base * channel_scale * row_scale).astype(jnp.bfloat16)


def strengthened(array, rng, source, target, parts, factor):
    owner, partner = [(jnp.arange(array.shape[axis_at]) // (array.shape[axis_at] // parts)).reshape([-1 if axis == axis_at else 1 for axis in range(array.ndim)]) for axis_at in (source, target)]
    chosen = jax.random.permutation(rng, parts)[partner]
    strong = (owner == chosen) | (owner == (partner + parts // 2) % parts)
    return jnp.where(strong, factor * array, array)


def block_levels(stream_key, shape, cuts, smallest, largest):
    def one(position, blocks):
        steps = jax.random.uniform(jax.random.fold_in(jax.random.fold_in(stream_key, 6), position), (blocks,), jnp.float32, smallest / len(cuts), largest / len(cuts))
        return jnp.repeat(jnp.exp(steps), shape[position] // blocks).reshape((-1,) + (1,) * (len(shape) - position - 1))

    factor_of = one(*cuts[0])
    for cut in cuts[1:]:
        factor_of = factor_of * one(*cut)
    return factor_of


def scatter_about(key, extent, spread, reach, pieces=(), kind=jnp.bfloat16):
    values = jax.random.normal(key, extent, jnp.float32) * spread
    if len(pieces) > 0:
        values = block_levels(key, extent, pieces, -0.22, 0.18) * values
    return jnp.clip(values, min=-reach, max=reach).astype(kind)


def noise_with(rng, dims, width, limit, pieces, heavy, dtype=jnp.bfloat16):
    values = width * jax.random.normal(rng, dims, jnp.float32)
    if pieces:
        values = values * block_levels(rng, dims, pieces, -0.22, 0.18)
    return jnp.clip(strengthened(values, jax.random.fold_in(rng, 3), *heavy), -limit, limit).astype(dtype)


def setup_inputs(seed: int = 0) -> dict:
    key_list = jax.random.split(jax.random.key(seed), 9)
    activations = draw_activations(jax.random.fold_in(key_list[8], 71), 0)
    first_factor = scatter_about(key_list[1], (B, B), B ** -0.5, 0.25)
    spectral = scatter_about(key_list[2], (C, TOKENS), 1.0, 4.0, ((0, 8), (1, 16)), jnp.float32)
    second_factor = scatter_about(key_list[3], (A, A), A ** -0.5, 0.375, (), jnp.float32)
    gate_scale = scatter_about(key_list[4], (C,), 1.0, 4.0, (), jnp.float32)
    gate_shift = scatter_about(key_list[5], (C,), 1.0, 4.0, (), jnp.float32)
    expand_weight = scatter_about(key_list[6], (C, H), C ** -0.5, 0.1875, ((1, 128),))
    reduce_weight = noise_with(key_list[7], (H, C), H ** -0.5, 0.3125, ((0, 128),), (0, 1, 128, 5.5))
    return {"activations": activations, "first_factor": first_factor, "spectral": spectral, "second_factor": second_factor, "gate_scale": gate_scale, "gate_shift": gate_shift, "expand_weight": expand_weight, "reduce_weight": reduce_weight}


epsilon = 1e-06

def reference(activations, first_factor, spectral, second_factor, gate_scale, gate_shift, expand_weight, reduce_weight):
    inputs = activations.astype(jnp.float32)
    blocks = inputs.reshape(C, A, B)
    first_pass = jnp.einsum('cai,ij->caj', blocks, first_factor.astype(jnp.float32))
    spectrum = first_pass * spectral.reshape(C, A, B)
    mixed = jnp.einsum('pa,caj->cpj', second_factor, spectrum, precision=lax.Precision.HIGHEST)
    gating = jax.nn.sigmoid(inputs * gate_scale[:, None] + gate_shift[:, None])
    residual_in = (inputs + gating * mixed.reshape(C, A * B)).astype(jnp.bfloat16)
    tile_width = A * B // DEVICES
    token_tiles = residual_in.reshape(C, DEVICES, tile_width).transpose(1, 0, 2)

    def apply_layer(columns):
        values = columns.astype(jnp.float32)
        scale = lax.rsqrt(lax.optimization_barrier(jnp.mean(values * values, axis=0, keepdims=True)) + epsilon)
        normed = (values * scale).astype(jnp.bfloat16)
        hidden = jax.nn.gelu(jnp.dot(expand_weight.T, normed, preferred_element_type=jnp.float32)).astype(jnp.bfloat16)
        mlp_out = jnp.dot(reduce_weight.T, hidden, preferred_element_type=jnp.float32)
        return (values + mlp_out).astype(jnp.bfloat16)
    results = lax.map(apply_layer, token_tiles)
    return results.transpose(1, 0, 2).reshape(C, A * B)
```

```python
import functools

import jax
import jax.numpy as jnp
from jax import lax
from jax.experimental import pallas as pl
from jax.experimental.pallas import tpu as pltpu
from jax.sharding import PartitionSpec as P

MESH = pl.DeviceIdType.MESH
NC = 2
CH = 128 // NC
CP = 8 // NC
TB = 256
NT = 1024 // TB
LANES = 128
ORDERS = (("x", "y", "z"), ("y", "z", "x"), ("z", "x", "y"))
epsilon = 1e-06
f32, bf16 = jnp.float32, jnp.bfloat16


def kernel(
    act, f1, spec, f2, scale, shift, we, wr, out,
    act_v, f1_v, spec_v, f2_v, f2_b, sc_v, sh_v, sc_t, sh_t,
    we_all, wr_s, wr_t, x32, s_send, s_recv, m_send, m_recv, r_send, r_recv,
    n_all, h_buf, p_send, p_recv, o_send,
    in_sem, w_sem, own_sem, a1s, a1r, a2s, a2r, a3s, a3r, a4s, a4r, ns, nr, ps, pr,
    g1s, g1r, g2s, g2r, g3s, g3r,
):
    seq = lax.axis_index("seq")
    ten = lax.axis_index("tensor")
    core = seq % 2
    z = (seq // 2) % 4
    y_lo = seq // 8
    x = ten // 2
    y = (ten % 2) * 2 + y_lo
    pos = {"x": x, "y": y, "z": z}

    def at(axis, step):
        p = dict(pos)
        p[axis] = (p[axis] + step) % 4
        return ((p["y"] % 2) * 8 + p["z"] * 2 + core, p["x"] * 2 + p["y"] // 2)

    partner = (seq + 1 - 2 * core, ten)

    def remote(src, dst, s, r, dev):
        return pltpu.make_async_remote_copy(
            src_ref=src, dst_ref=dst, send_sem=s, recv_sem=r, device_id=dev, device_id_type=MESH
        )

    ins = [
        pltpu.make_async_copy(a, b, in_sem.at[i])
        for i, (a, b) in enumerate(
            ((act, act_v), (f1, f1_v), (spec, spec_v), (f2, f2_v), (scale, sc_v), (shift, sh_v))
        )
    ]
    wins = []
    for i, (d1, d2, d3) in enumerate(ORDERS):
        row = (pos[d3] * 16 + pos[d2] * 4 + pos[d1]) * 16
        row_s = (pos[d2] * 4 + pos[d1]) * 16
        wins.append(pltpu.make_async_copy(
            we.at[pl.ds(16 * i, 16)], we_all.at[i, pl.ds(pl.multiple_of(row, 16), 16)], w_sem.at[i, 0]))
        wins.append(pltpu.make_async_copy(
            wr.at[pl.ds(16 * i, 16)], wr_s.at[i, pl.ds(pl.multiple_of(row_s, 16), 16)], w_sem.at[i, 1]))
    for c in wins + ins:
        c.start()

    barrier = pltpu.get_barrier_semaphore()
    for r in range(1, 16):
        pl.semaphore_signal(barrier, inc=1, device_id=((seq + r) % 16, ten), device_id_type=MESH)
    for r in range(1, 8):
        pl.semaphore_signal(barrier, inc=1, device_id=(seq, (ten + r) % 8), device_id_type=MESH)
    diagonal = ((1 - y_lo) * 8 + z * 2 + core, x * 2 + 1 - ten % 2)
    pl.semaphore_signal(barrier, inc=1, device_id=diagonal, device_id_type=MESH)
    pl.semaphore_wait(barrier, 23)

    def gather_copies(stage):
        sem_s, sem_r = ((g1s, g1r), (g2s, g2r))[stage]
        copies = []
        for i, (d1, d2, d3) in enumerate(ORDERS):
            n = (16, 64)[stage]
            base = pos[d2] * 4 + (pos[d1] if stage == 0 else 0)
            row = pl.multiple_of((pos[d3] * 16 + base) * 16, n)
            row_s = pl.multiple_of(base * 16, n)
            for step in (1, 2, 3):
                dev = at((d1, d2)[stage], step)
                a = we_all.at[i, pl.ds(row, n)]
                b = wr_s.at[i, pl.ds(row_s, n)]
                copies.append(remote(a, a, sem_s.at[i, step - 1, 0], sem_r.at[i, step - 1, 0], dev))
                copies.append(remote(b, b, sem_s.at[i, step - 1, 1], sem_r.at[i, step - 1, 1], dev))
        return copies

    def block_copies(which):
        copies = []
        for i, (d1, d2, d3) in enumerate(ORDERS):
            p = pos[d3]
            if which == 0:
                for q, step in ((0, 1), (1, 3)):
                    dev = at(d3, step)
                    a = we_all.at[i, pl.ds(pl.multiple_of(p * 256, 256), 256)]
                    b = wr_t.at[i, :, pl.ds(pl.multiple_of(p * 256, 256), 256)]
                    copies.append(remote(a, a, g3s.at[i, q, 0], g3r.at[i, q, 0], dev))
                    copies.append(remote(b, b, g3s.at[i, q, 1], g3r.at[i, q, 1], dev))
            else:
                for q, source, step in ((0, 3, 1), (1, 1, 3)):
                    dev = at(d3, step)
                    o = (p + source) % 4 * 256
                    a = we_all.at[i, pl.ds(pl.multiple_of(o + 128 * q, 128), 128)]
                    b = wr_t.at[i, pl.ds(512 * q, 512), pl.ds(pl.multiple_of(o, 256), 256)]
                    copies.append(remote(a, a, g3s.at[i, 2 + q, 0], g3r.at[i, 2 + q, 0], dev))
                    copies.append(remote(b, b, g3s.at[i, 2 + q, 1], g3r.at[i, 2 + q, 1], dev))
        return copies

    for c in wins:
        c.wait()
    g1 = gather_copies(0)
    for c in g1:
        c.start()
    for c in ins:
        c.wait()

    sc_t[...] = jnp.broadcast_to(sc_v[pl.ds(ten, 1), :], (LANES, LANES)).T
    sh_t[...] = jnp.broadcast_to(sh_v[pl.ds(ten, 1), :], (LANES, LANES)).T
    f2_b[...] = f2_v[...].astype(bf16)

    def first(a, _):
        cols = pl.ds(pl.multiple_of(a * 512, 512), 512)
        value = jnp.dot(act_v[:, cols], f1_v[...], preferred_element_type=f32) * spec_v[:, cols]
        for g in range(4):
            x32[g, pl.ds(a, 128, stride=16), :] = value[:, g * LANES:(g + 1) * LANES]
        return 0

    lax.fori_loop(0, 16, first, 0)

    def a1_copy(k, r):
        to = (seq + r) % 16
        return remote(
            s_send.at[pl.ds(CH * k + CP * to, CP)],
            s_recv.at[pl.ds(CP * k, CP), pl.ds(pl.multiple_of(16 * seq, 16), 16), :],
            a1s.at[k, r], a1r.at[k, r], (to, ten))

    def a1_own(k):
        return pltpu.make_async_copy(
            s_send.at[pl.ds(CH * k + CP * seq, CP)],
            s_recv.at[pl.ds(CP * k, CP), pl.ds(pl.multiple_of(16 * seq, 16), 16), :],
            own_sem.at[0, k])

    def a2_copy(k, r):
        to = (seq + r) % 16
        return remote(
            m_send.at[pl.ds(CP * k, CP), pl.ds(pl.multiple_of(16 * to, 16), 16), :],
            m_recv.at[pl.ds(CH * k + CP * seq, CP)],
            a2s.at[k, r], a2r.at[k, r], (to, ten))

    def a2_own(k):
        return pltpu.make_async_copy(
            m_send.at[pl.ds(CP * k, CP), pl.ds(pl.multiple_of(16 * seq, 16), 16), :],
            m_recv.at[pl.ds(CH * k + CP * seq, CP)],
            own_sem.at[1, k])

    def a3_refs(k, to):
        src = r_send.at[pl.ds(CH * k, CH), pl.ds(pl.multiple_of(to * 1024, 1024), 1024)]
        dst = r_recv.at[pl.ds(pl.multiple_of(128 * ten + CH * k, CH), CH)]
        return src, dst

    def a3_copy(k, r):
        to = (ten + r) % 8
        src, dst = a3_refs(k, to)
        return remote(src, dst, a3s.at[k, r], a3r.at[k, r], (seq, to))

    def a3_own(k):
        src, dst = a3_refs(k, ten)
        return pltpu.make_async_copy(src, dst, own_sem.at[2, k])

    def a4_refs(b, to):
        src = o_send.at[b, pl.ds(pl.multiple_of(to * 128, 128), 128)]
        dst = out.at[:, pl.ds(pl.multiple_of(ten * 1024 + b * TB, TB), TB)]
        return src, dst

    def a4_copy(b, r):
        to = (ten + r) % 8
        src, dst = a4_refs(b, to)
        return remote(src, dst, a4s.at[b, r], a4r.at[b, r], (seq, to))

    def a4_own(b):
        src, dst = a4_refs(b, ten)
        return pltpu.make_async_copy(src, dst, a4s.at[b, 0])

    def loop(lo, hi, body):
        def step(i, _):
            body(i)
            return 0
        lax.fori_loop(lo, hi, step, 0)

    for k in range(NC):
        def cast(n, k=k):
            c = CH * k + 8 * n
            for g in range(4):
                rows = x32[g, pl.ds(pl.multiple_of(c * 16, 128), 128), :]
                s_send[pl.ds(c, 8), :, g * LANES:(g + 1) * LANES] = rows.astype(bf16).reshape(8, 16, LANES)
        loop(0, CH // 8, cast)
        a1_own(k).start()
        loop(1, 16, lambda r, k=k: a1_copy(k, r).start())

    for c in g1:
        c.wait_recv()
    g2 = gather_copies(1)
    for c in g2:
        c.start()
    for c in g2:
        c.wait_recv()
    for i, (d1, d2, d3) in enumerate(ORDERS):
        col = pl.ds(pl.multiple_of(pos[d3] * 256, 256), 256)
        def turn(n, i=i, col=col):
            c = pl.multiple_of(n * 256, 256)
            wr_t[i, pl.ds(c, 256), col] = wr_s[i, :, pl.ds(c, 256)].astype(f32).T.astype(bf16)
        loop(0, 4, turn)
    g3 = block_copies(0)
    for c in g3:
        c.start()

    for k in range(NC):
        a1_own(k).wait()
        loop(1, 16, lambda r, k=k: a1_copy(k, r).wait_recv())
        def mix(n, k=k):
            c = CP * k + n
            m_send[c] = jnp.dot(f2_b[...], s_recv[c], preferred_element_type=f32).astype(bf16)
        loop(0, CP, mix)
        a2_own(k).start()
        loop(1, 16, lambda r, k=k: a2_copy(k, r).start())

    for c in g3:
        c.wait_recv()
    g4 = block_copies(1)
    for c in g4:
        c.start()

    for k in range(NC):
        a2_own(k).wait()
        loop(1, 16, lambda r, k=k: a2_copy(k, r).wait_recv())
        def widen(n, k=k):
            c = CH * k + 8 * n
            rows = m_recv[pl.ds(c, 8)].astype(f32).reshape(128, 512)
            for g in range(4):
                x32[g, pl.ds(pl.multiple_of(c * 16, 128), 128), :] = rows[:, g * LANES:(g + 1) * LANES]
        loop(0, CH // 8, widen)
        chans = pl.ds(CH * k, CH)
        def gate(p, k=k, chans=chans):
            for g in range(4):
                cols = pl.ds(pl.multiple_of(p * 512 + g * LANES, LANES), LANES)
                mixed = x32[g, pl.ds(CH * k * 16 + p, CH, stride=16), :]
                value = act_v[chans, cols].astype(f32)
                gating = jax.nn.sigmoid(value * sc_t[chans, :] + sh_t[chans, :])
                r_send[chans, cols] = (value + gating * mixed).astype(bf16)
        loop(0, 16, gate)
        a3_own(k).start()
        loop(1, 8, lambda r, k=k: a3_copy(k, r).start())

    for k in range(NC):
        a3_own(k).wait()
        loop(1, 8, lambda r, k=k: a3_copy(k, r).wait_recv())

    def norm_copy(b):
        cols = pl.ds(pl.multiple_of(b * TB, TB), TB)
        return remote(n_all.at[0, :, cols], n_all.at[1, :, cols], ns.at[b], nr.at[b], partner)

    def normalize(b):
        cols = pl.ds(pl.multiple_of(b * TB, TB), TB)
        def square(n, total):
            v = r_recv[pl.ds(pl.multiple_of(n * 64, 64), 64), cols].astype(f32)
            return total + jnp.sum((v * v).reshape(8, 8, TB), axis=0)
        total = lax.fori_loop(0, 16, square, jnp.zeros((8, TB), f32))
        factor = lax.rsqrt(jnp.sum(total, axis=0, keepdims=True) * (1.0 / 1024) + epsilon)
        def write(n):
            rows = pl.ds(pl.multiple_of(n * 64, 64), 64)
            n_all[0, rows, cols] = (r_recv[rows, cols].astype(f32) * factor).astype(bf16)
        loop(0, 16, write)
        norm_copy(b).start()

    loop(0, NT, normalize)

    for c in g4:
        c.wait_recv()

    def mlp(which, cols):
        tokens = n_all[which, :, cols]
        for i in range(3):
            product = jnp.dot(we_all[i], tokens, preferred_element_type=f32)
            h_buf[i] = jax.nn.gelu(product).astype(bf16)
        total = jnp.dot(wr_t[0], h_buf[0], preferred_element_type=f32)
        for i in (1, 2):
            total += jnp.dot(wr_t[i], h_buf[i], preferred_element_type=f32)
        return total

    def part_copy(b):
        return remote(p_send.at[b], p_recv.at[b], ps.at[b], pr.at[b], partner)

    def theirs(b):
        norm_copy(b).wait_recv()
        cols = pl.ds(pl.multiple_of(b * TB, TB), TB)
        p_send[b] = mlp(1, cols).astype(bf16)
        part_copy(b).start()

    loop(0, NT, theirs)

    def ours(b):
        cols = pl.ds(pl.multiple_of(b * TB, TB), TB)
        total = mlp(0, cols)
        part_copy(b).wait_recv()
        o_send[b] = (r_recv[:, cols].astype(f32) + (total + p_recv[b].astype(f32))).astype(bf16)
        a4_own(b).start()
        loop(1, 8, lambda r: a4_copy(b, r).start())

    loop(0, NT, ours)

    def drain(b):
        a4_own(b).wait()
        loop(1, 8, lambda r: a4_copy(b, r).wait_recv())
        loop(1, 8, lambda r: a4_copy(b, r).wait_send())
        norm_copy(b).wait_send()
        part_copy(b).wait_send()
    loop(0, NT, drain)
    for c in g1 + g2 + g3 + g4:
        c.wait_send()
    for k in range(NC):
        loop(1, 16, lambda r, k=k: a1_copy(k, r).wait_send())
        loop(1, 16, lambda r, k=k: a2_copy(k, r).wait_send())
        loop(1, 8, lambda r, k=k: a3_copy(k, r).wait_send())


def on_device(act, f1, spec, f2, scale, shift, we, wr):
    vmem, dma = pltpu.VMEM, pltpu.SemaphoreType.DMA
    scratch = [
        vmem((128, 8192), bf16), vmem((512, 512), bf16), vmem((128, 8192), f32), vmem((256, 256), f32),
        vmem((256, 256), bf16), vmem((8, 128), f32), vmem((8, 128), f32),
        vmem((128, 128), f32), vmem((128, 128), f32),
        vmem((3, 1024, 1024), bf16), vmem((3, 256, 1024), bf16), vmem((3, 1024, 1024), bf16),
        vmem((4, 2048, 128), f32),
        vmem((128, 16, 512), bf16), vmem((8, 256, 512), bf16),
        vmem((8, 256, 512), bf16), vmem((128, 16, 512), bf16),
        vmem((128, 8192), bf16), vmem((1024, 1024), bf16),
        vmem((2, 1024, 1024), bf16), vmem((3, 1024, TB), bf16),
        vmem((NT, 1024, TB), bf16), vmem((NT, 1024, TB), bf16), vmem((NT, 1024, TB), bf16),
        dma((6,)), dma((3, 2)), dma((3, NC)),
        dma((NC, 16)), dma((NC, 16)), dma((NC, 16)), dma((NC, 16)),
        dma((NC, 8)), dma((NC, 8)), dma((NT, 8)), dma((NT, 8)),
        dma((NT,)), dma((NT,)), dma((NT,)), dma((NT,)),
        dma((3, 3, 2)), dma((3, 3, 2)), dma((3, 3, 2)), dma((3, 3, 2)), dma((3, 4, 2)), dma((3, 4, 2)),
    ]
    return pl.pallas_call(
        kernel,
        out_shape=jax.ShapeDtypeStruct((128, 8192), bf16),
        in_specs=[pl.BlockSpec(memory_space=pl.ANY)] * 8,
        out_specs=pl.BlockSpec(memory_space=pl.ANY),
        scratch_shapes=scratch,
        compiler_params=pltpu.CompilerParams(
            collective_id=0, has_side_effects=True, vmem_limit_bytes=67_043_328),
        name="mixer",
    )(act, f1, spec, f2, scale.reshape(8, 128), shift.reshape(8, 128), we.T, wr)


def solution(mesh):
    return jax.shard_map(
        on_device,
        mesh=mesh,
        in_specs=(
            P("tensor", "seq"),
            P(),
            P("tensor", "seq"),
            P(),
            P(),
            P(),
            P(None, ("seq", "tensor")),
            P(("seq", "tensor"), None),
        ),
        out_specs=P("tensor", "seq"),
        check_vma=False,
    )
```

```python
import functools

import jax
import jax.numpy as jnp
from jax import lax
from jax.experimental import pallas as pl
from jax.experimental.pallas import tpu as pltpu
from jax.sharding import PartitionSpec as P

MESH = pl.DeviceIdType.MESH
NK = 2
W = 512 // NK
TB = 256
NT = 4
LANES = 128
ORDERS = (("y", "z", "x"), ("y", "x", "z"), ("y", "z", "x"))
TURNED = (True, False, True)
epsilon = 1e-06
f32, bf16 = jnp.float32, jnp.bfloat16


def kernel(
    act, f1, spec, f2, scale, shift, we, wr, out,
    act_v, f1_v, spec_v, f2_v, f2_b, sc_v, sh_v, sc_t, sh_t,
    we_all, wr_s, wr_t, x32, s_send, s_recv, m_send, m_recv, r_send, r_recv,
    n_all, acc, h_buf, p_send, p_recv, o_send,
    in_sem, w_sem, own_sem, a1s, a1r, a2s, a2r, a3s, a3r, a4s, a4r, ns, nr, ps, pr,
    g1s, g1r, g2s, g2r, g3s, g3r,
):
    seq = lax.axis_index("seq")
    ten = lax.axis_index("tensor")
    core = seq % 2
    z = (seq // 2) % 4
    y_lo = seq // 8
    x = ten // 2
    y = (ten % 2) * 2 + y_lo
    pos = {"x": x, "y": y, "z": z}

    def at(axis, step):
        p = dict(pos)
        p[axis] = (p[axis] + step) % 4
        return ((p["y"] % 2) * 8 + p["z"] * 2 + core, p["x"] * 2 + p["y"] // 2)

    partner = (seq + 1 - 2 * core, ten)

    def remote(src, dst, s, r, dev):
        return pltpu.make_async_remote_copy(
            src_ref=src, dst_ref=dst, send_sem=s, recv_sem=r, device_id=dev, device_id_type=MESH
        )

    ins = [
        pltpu.make_async_copy(a, b, in_sem.at[i])
        for i, (a, b) in enumerate(
            ((act, act_v), (f1, f1_v), (spec, spec_v), (f2, f2_v), (scale, sc_v), (shift, sh_v))
        )
    ]
    wins = []
    for i, (d1, d2, d3) in enumerate(ORDERS):
        row = (pos[d3] * 16 + pos[d2] * 4 + pos[d1]) * 16
        wins.append(pltpu.make_async_copy(
            we.at[pl.ds(16 * i, 16)], we_all.at[i, pl.ds(pl.multiple_of(row, 16), 16)], w_sem.at[i, 0]))
        wins.append(pltpu.make_async_copy(
            wr.at[pl.ds(16 * i, 16)], wr_s.at[i, pos[d2], pos[d1]], w_sem.at[i, 1]))
    for c in wins + ins:
        c.start()

    barrier = pltpu.get_barrier_semaphore()
    for r in range(1, 16):
        pl.semaphore_signal(barrier, inc=1, device_id=((seq + r) % 16, ten), device_id_type=MESH)
    for r in range(1, 8):
        pl.semaphore_signal(barrier, inc=1, device_id=(seq, (ten + r) % 8), device_id_type=MESH)
    diagonal = ((1 - y_lo) * 8 + z * 2 + core, x * 2 + 1 - ten % 2)
    pl.semaphore_signal(barrier, inc=1, device_id=diagonal, device_id_type=MESH)

    def gather_copies(stage, i):
        sem_s, sem_r = ((g1s, g1r), (g2s, g2r))[stage]
        d1, d2, d3 = ORDERS[i]
        n = (16, 64)[stage]
        base = pos[d2] * 4 + (pos[d1] if stage == 0 else 0)
        a = we_all.at[i, pl.ds(pl.multiple_of((pos[d3] * 16 + base) * 16, n), n)]
        if stage == 0:
            b = wr_s.at[i, pos[d2], pos[d1]]
        elif TURNED[i]:
            b = wr_s.at[i, :, pos[d1]]
        else:
            b = wr_s.at[i, pos[d2]]
        copies = []
        for step in (1, 3, 2):
            dev = at((d1, d2)[stage], step)
            copies.append(remote(a, a, sem_s.at[i, step - 1, 0], sem_r.at[i, step - 1, 0], dev))
            dev = at((d1, d2)[1 - stage if TURNED[i] else stage], step)
            copies.append(remote(b, b, sem_s.at[i, step - 1, 1], sem_r.at[i, step - 1, 1], dev))
        return copies

    def block_copies(which, i):
        d3 = ORDERS[i][2]
        p = pos[d3]
        copies = []
        if which == 0:
            a = we_all.at[i, pl.ds(pl.multiple_of(p * 256, 256), 256)]
            b = wr_t.at[i, :, pl.ds(pl.multiple_of(p * 256, 256), 256)]
            for q, step in ((0, 1), (1, 3)):
                dev = at(d3, step)
                copies.append(remote(a, a, g3s.at[i, q, 0], g3r.at[i, q, 0], dev))
                copies.append(remote(b, b, g3s.at[i, q, 1], g3r.at[i, q, 1], dev))
        else:
            for q, source, step in ((0, 3, 1), (1, 1, 3)):
                dev = at(d3, step)
                o = (p + source) % 4 * 256
                a = we_all.at[i, pl.ds(pl.multiple_of(o + 128 * q, 128), 128)]
                b = wr_t.at[i, pl.ds(512 * q, 512), pl.ds(pl.multiple_of(o, 256), 256)]
                copies.append(remote(a, a, g3s.at[i, 2 + q, 0], g3r.at[i, 2 + q, 0], dev))
                copies.append(remote(b, b, g3s.at[i, 2 + q, 1], g3r.at[i, 2 + q, 1], dev))
        return copies

    g1 = [gather_copies(0, i) for i in range(3)]
    g2 = [gather_copies(1, i) for i in range(3)]
    g3 = [block_copies(0, i) for i in range(3)]
    g4 = [block_copies(1, i) for i in range(3)]

    def start(copies):
        for c in copies:
            c.start()

    def arrive(copies):
        for c in copies:
            c.wait_recv()

    def loop(lo, hi, body, unroll=1):
        def step(i, _):
            body(i)
            return 0
        lax.fori_loop(lo, hi, step, 0, unroll=unroll)

    def turn(i):
        col = pl.ds(pl.multiple_of(pos[ORDERS[i][2]] * 256, 256), 256)
        def piece(n):
            c = pl.multiple_of(n * 256, 256)
            rows = wr_s[i, :, :, :, pl.ds(c, 256)].astype(f32).reshape(256, 256)
            wr_t[i, pl.ds(c, 256), col] = rows.T.astype(bf16)
        loop(0, 4, piece)

    def a1_refs(k, to):
        src = s_send.at[k, pl.ds(8 * to, 8)]
        dst = s_recv.at[k, :, pl.ds(pl.multiple_of(16 * seq, 16), 16), :]
        return src, dst

    def a1_copy(k, r):
        to = (seq + r) % 16
        src, dst = a1_refs(k, to)
        return remote(src, dst, a1s.at[k, r], a1r.at[k, r], (to, ten))

    def a1_own(k):
        src, dst = a1_refs(k, seq)
        return pltpu.make_async_copy(src, dst, own_sem.at[0, k])

    def a2_refs(k, to):
        src = m_send.at[k, :, pl.ds(pl.multiple_of(16 * to, 16), 16), :]
        dst = m_recv.at[k, pl.ds(8 * seq, 8)]
        return src, dst

    def a2_copy(k, r):
        to = (seq + r) % 16
        src, dst = a2_refs(k, to)
        return remote(src, dst, a2s.at[k, r], a2r.at[k, r], (to, ten))

    def a2_own(k):
        src, dst = a2_refs(k, seq)
        return pltpu.make_async_copy(src, dst, own_sem.at[1, k])

    def a3_refs(k, to):
        src = r_send.at[k, to]
        dst = r_recv.at[pl.ds(2 * k, 2), pl.ds(pl.multiple_of(128 * ten, 128), 128)]
        return src, dst

    def a3_copy(k, r):
        to = (ten + r) % 8
        src, dst = a3_refs(k, to)
        return remote(src, dst, a3s.at[k, r], a3r.at[k, r], (seq, to))

    def a3_own(k):
        src, dst = a3_refs(k, ten)
        return pltpu.make_async_copy(src, dst, own_sem.at[2, k])

    def a4_refs(b, to):
        src = o_send.at[b, pl.ds(pl.multiple_of(to * 128, 128), 128)]
        dst = out.at[:, pl.ds(pl.multiple_of(ten * 1024 + (b % 2) * 512 + (b // 2) * TB, TB), TB)]
        return src, dst

    def a4_copy(b, r):
        to = (ten + r) % 8
        src, dst = a4_refs(b, to)
        return remote(src, dst, a4s.at[b, r], a4r.at[b, r], (seq, to))

    def a4_own(b):
        src, dst = a4_refs(b, ten)
        return pltpu.make_async_copy(src, dst, a4s.at[b, 0])

    for c in ins:
        c.wait()

    def first(k):
        def block(a):
            value = jnp.dot(
                act_v[:, pl.ds(pl.multiple_of(a * 512, 512), 512)], f1_v[:, W * k:W * (k + 1)],
                preferred_element_type=f32)
            value = value * spec_v[:, pl.ds(pl.multiple_of(a * 512 + W * k, W), W)]
            for g in range(W // LANES):
                x32[g, pl.ds(a, 128, stride=16), :] = value[:, g * LANES:(g + 1) * LANES]
        loop(0, 16, block, 4)

    def send_first(k):
        def cast(n):
            c = 8 * n
            for g in range(W // LANES):
                rows = x32[g, pl.ds(pl.multiple_of(c * 16, 128), 128), :]
                s_send[k, pl.ds(c, 8), :, g * LANES:(g + 1) * LANES] = rows.astype(bf16).reshape(8, 16, LANES)
        loop(0, 16, cast)
        a1_own(k).start()
        loop(1, 16, lambda r: a1_copy(k, r).start())

    first(0)
    pl.semaphore_wait(barrier, 23)
    for c in wins:
        c.wait()
    for i in range(3):
        start(g1[i])
    sc_t[...] = jnp.broadcast_to(sc_v[pl.ds(ten, 1), :], (LANES, LANES)).T
    sh_t[...] = jnp.broadcast_to(sh_v[pl.ds(ten, 1), :], (LANES, LANES)).T
    f2_b[...] = f2_v[...].astype(bf16)

    send_first(0)
    first(1)
    for i in range(3):
        arrive(g1[i])
        start(g2[i])

    def mixing(k):
        a1_own(k).wait()
        loop(1, 16, lambda r: a1_copy(k, r).wait_recv())
        if k == 0:
            send_first(1)
        def mix(c):
            m_send[k, c] = jnp.dot(f2_b[...], s_recv[k, c], preferred_element_type=f32).astype(bf16)
        loop(0, 8, mix)
        a2_own(k).start()
        loop(1, 16, lambda r: a2_copy(k, r).start())

    mixing(0)
    arrive(g2[0])
    turn(0)
    start(g3[0])
    mixing(1)
    for i in (1, 2):
        arrive(g2[i])
        turn(i)
        start(g3[i])

    def gating(k):
        a2_own(k).wait()
        loop(1, 16, lambda r: a2_copy(k, r).wait_recv())
        def widen(n):
            c = 8 * n
            rows = m_recv[k, pl.ds(c, 8)].astype(f32).reshape(128, W)
            for g in range(W // LANES):
                x32[g, pl.ds(pl.multiple_of(c * 16, 128), 128), :] = rows[:, g * LANES:(g + 1) * LANES]
        loop(0, 16, widen)
        def gate(p):
            for g in range(W // LANES):
                mixed = x32[g, pl.ds(p, 128, stride=16), :]
                cols = pl.ds(pl.multiple_of(p * 512 + W * k + g * LANES, LANES), LANES)
                value = act_v[:, cols].astype(f32)
                sig = jax.nn.sigmoid(value * sc_t[...] + sh_t[...])
                r_send[k, p // 2, p % 2, :, g * LANES:(g + 1) * LANES] = (value + sig * mixed).astype(bf16)
        loop(0, 16, gate)
        a3_own(k).start()
        loop(1, 8, lambda r: a3_copy(k, r).start())

    gating(0)
    arrive(g3[0])
    start(g4[0])
    gating(1)

    def norm_copy(b):
        return remote(n_all.at[0, b], n_all.at[1, b], ns.at[b], nr.at[b], partner)

    def normalize(b):
        def square(n, total):
            v = r_recv[b, pl.ds(pl.multiple_of(n * 64, 64), 64), :].astype(f32)
            return total + jnp.sum((v * v).reshape(8, 8, TB), axis=0)
        total = lax.fori_loop(0, 16, square, jnp.zeros((8, TB), f32))
        factor = lax.rsqrt(jnp.sum(total, axis=0, keepdims=True) * (1.0 / 1024) + epsilon)
        def write(n):
            rows = pl.ds(pl.multiple_of(n * 64, 64), 64)
            n_all[0, b, rows, :] = (r_recv[b, rows, :].astype(f32) * factor).astype(bf16)
        loop(0, 16, write)
        norm_copy(b).start()

    def mlp(i, blocks):
        for q, (which, b) in enumerate(blocks):
            product = jnp.dot(we_all[i], n_all[which, b], preferred_element_type=f32)
            h_buf[q] = jax.nn.gelu(product).astype(bf16)
        return [jnp.dot(wr_t[i], h_buf[q], preferred_element_type=f32) for q in range(2)]

    def part_copy(b):
        return remote(p_send.at[b], p_recv.at[b], ps.at[b], pr.at[b], partner)

    def opening(which, n):
        acc[which, 2 * n], acc[which, 2 * n + 1] = mlp(0, ((which, 2 * n), (which, 2 * n + 1)))

    def middle(b):
        part, total = mlp(1, ((1, b), (0, b)))
        acc[1, b] += part
        acc[0, b] += total

    def last(b):
        part, total = mlp(2, ((1, b), (0, b)))
        p_send[b] = (acc[1, b] + part).astype(bf16)
        part_copy(b).start()
        acc[0, b] += total

    def finish(b):
        part_copy(b).wait_recv()
        o_send[b] = (r_recv[b].astype(f32) + (acc[0, b] + p_recv[b].astype(f32))).astype(bf16)
        a4_own(b).start()
        loop(1, 8, lambda r: a4_copy(b, r).start())

    def settle(k):
        a3_own(k).wait()
        loop(1, 8, lambda r: a3_copy(k, r).wait_recv())
        loop(2 * k, 2 * k + 2, normalize)

    settle(0)
    arrive(g3[1])
    start(g4[1])
    arrive(g4[0])
    loop(0, 1, lambda n: opening(0, n))
    loop(0, 2, lambda b: norm_copy(b).wait_recv())
    loop(0, 1, lambda n: opening(1, n))
    arrive(g3[2])
    start(g4[2])
    settle(1)
    loop(1, 2, lambda n: opening(0, n))
    loop(2, 4, lambda b: norm_copy(b).wait_recv())
    loop(1, 2, lambda n: opening(1, n))
    arrive(g4[1])
    loop(0, 2, middle)
    arrive(g4[2])
    last(0)
    last(1)
    finish(0)
    def tail(b):
        middle(b)
        last(b)
        finish(b - 1)
    loop(2, NT, tail)
    finish(NT - 1)

    def drain(b):
        a4_own(b).wait()
        loop(1, 8, lambda r: a4_copy(b, r).wait_recv())
        loop(1, 8, lambda r: a4_copy(b, r).wait_send())
        norm_copy(b).wait_send()
        part_copy(b).wait_send()
    loop(0, NT, drain)
    for i in range(3):
        for c in g1[i] + g2[i] + g3[i] + g4[i]:
            c.wait_send()
    for k in range(NK):
        loop(1, 16, lambda r, k=k: a1_copy(k, r).wait_send())
        loop(1, 16, lambda r, k=k: a2_copy(k, r).wait_send())
        loop(1, 8, lambda r, k=k: a3_copy(k, r).wait_send())


def on_device(act, f1, spec, f2, scale, shift, we, wr):
    vmem, dma = pltpu.VMEM, pltpu.SemaphoreType.DMA
    scratch = [
        vmem((128, 8192), bf16), vmem((512, 512), bf16), vmem((128, 8192), f32), vmem((256, 256), f32),
        vmem((256, 256), bf16), vmem((8, 128), f32), vmem((8, 128), f32),
        vmem((128, 128), f32), vmem((128, 128), f32),
        vmem((3, 1024, 1024), bf16), vmem((3, 4, 4, 16, 1024), bf16), vmem((3, 1024, 1024), bf16),
        vmem((W // 128, 2048, 128), f32),
        vmem((NK, 128, 16, W), bf16), vmem((NK, 8, 256, W), bf16),
        vmem((NK, 8, 256, W), bf16), vmem((NK, 128, 16, W), bf16),
        vmem((NK, 8, 2, 128, W), bf16), vmem((NT, 1024, TB), bf16),
        vmem((2, NT, 1024, TB), bf16), vmem((2, NT, 1024, TB), f32), vmem((2, 1024, TB), bf16),
        vmem((NT, 1024, TB), bf16), vmem((NT, 1024, TB), bf16), vmem((NT, 1024, TB), bf16),
        dma((6,)), dma((3, 2)), dma((3, NK)),
        dma((NK, 16)), dma((NK, 16)), dma((NK, 16)), dma((NK, 16)),
        dma((NK, 8)), dma((NK, 8)), dma((NT, 8)), dma((NT, 8)),
        dma((NT,)), dma((NT,)), dma((NT,)), dma((NT,)),
        dma((3, 3, 2)), dma((3, 3, 2)), dma((3, 3, 2)), dma((3, 3, 2)), dma((3, 4, 2)), dma((3, 4, 2)),
    ]
    return pl.pallas_call(
        kernel,
        out_shape=jax.ShapeDtypeStruct((128, 8192), bf16),
        in_specs=[pl.BlockSpec(memory_space=pl.ANY)] * 8,
        out_specs=pl.BlockSpec(memory_space=pl.ANY),
        scratch_shapes=scratch,
        compiler_params=pltpu.CompilerParams(
            collective_id=0, has_side_effects=True, vmem_limit_bytes=67_043_328),
        name="mixer",
    )(act, f1, spec, f2, scale.reshape(8, 128), shift.reshape(8, 128), we.T, wr)


def solution(mesh):
    return jax.shard_map(
        on_device,
        mesh=mesh,
        in_specs=(
            P("tensor", "seq"),
            P(),
            P("tensor", "seq"),
            P(),
            P(),
            P(),
            P(None, ("seq", "tensor")),
            P(("seq", "tensor"), None),
        ),
        out_specs=P("tensor", "seq"),
        check_vma=False,
    )
```

```python
import functools

import jax
import jax.numpy as jnp
from jax import lax
from jax.experimental import pallas as pl
from jax.experimental.pallas import tpu as pltpu
from jax.sharding import PartitionSpec as P

MESH = pl.DeviceIdType.MESH
NK = 2
W = 512 // NK
TB = 256
NT = 4
LANES = 128
ORDERS = (("y", "z", "x"), ("y", "x", "z"), ("y", "z", "x"))
WE_PATHS = (("y", "z", "x"), ("y", "x", "z"), ("z", "x", "y"))
WR_PATHS = (("z", "y", "x"), ("y", "x", "z"), ("y", "z", "x"))
epsilon = 1e-06
f32, bf16 = jnp.float32, jnp.bfloat16


def kernel(
    act, f1, spec, f2, scale, shift, we, wr, out,
    act_v, f1_v, spec_v, f2_v, f2_b, sc_v, sh_v, sc_t, sh_t,
    we_all, wr_s, wr_t, x32, s_send, s_recv, m_send, m_recv, r_send, r_recv,
    n_all, acc, h_buf, p_send, p_recv, o_send,
    in_sem, w_sem, own_sem, a1s, a1r, a2s, a2r, a3s, a3r, a4s, a4r, ns, nr, ps, pr,
    g1s, g1r, g2s, g2r, g3s, g3r,
):
    seq = lax.axis_index("seq")
    ten = lax.axis_index("tensor")
    core = seq % 2
    z = (seq // 2) % 4
    y_lo = seq // 8
    x = ten // 2
    y = (ten % 2) * 2 + y_lo
    pos = {"x": x, "y": y, "z": z}

    def at(axis, step):
        p = dict(pos)
        p[axis] = (p[axis] + step) % 4
        return ((p["y"] % 2) * 8 + p["z"] * 2 + core, p["x"] * 2 + p["y"] // 2)

    partner = (seq + 1 - 2 * core, ten)

    def remote(src, dst, s, r, dev):
        return pltpu.make_async_remote_copy(
            src_ref=src, dst_ref=dst, send_sem=s, recv_sem=r, device_id=dev, device_id_type=MESH
        )

    ins = [
        pltpu.make_async_copy(a, b, in_sem.at[i])
        for i, (a, b) in enumerate(
            ((act, act_v), (f1, f1_v), (spec, spec_v), (f2, f2_v), (scale, sc_v), (shift, sh_v))
        )
    ]
    wins = []
    for i, (d1, d2, d3) in enumerate(ORDERS):
        wins.append(pltpu.make_async_copy(
            we.at[pl.ds(16 * i, 16)], we_all.at[i, pos[d3], pos[d2], pos[d1]], w_sem.at[i, 0]))
        wins.append(pltpu.make_async_copy(
            wr.at[pl.ds(16 * i, 16)], wr_s.at[i, pos[d2], pos[d1]], w_sem.at[i, 1]))
    for c in wins + ins:
        c.start()

    barrier = pltpu.get_barrier_semaphore()
    for r in range(1, 16):
        pl.semaphore_signal(barrier, inc=1, device_id=((seq + r) % 16, ten), device_id_type=MESH)
    for r in range(1, 8):
        pl.semaphore_signal(barrier, inc=1, device_id=(seq, (ten + r) % 8), device_id_type=MESH)
    diagonal = ((1 - y_lo) * 8 + z * 2 + core, x * 2 + 1 - ten % 2)
    pl.semaphore_signal(barrier, inc=1, device_id=diagonal, device_id_type=MESH)

    def gather_copies(stage, i):
        sem_s, sem_r = ((g1s, g1r), (g2s, g2r))[stage]
        d1, d2, d3 = ORDERS[i]
        done = WE_PATHS[i][:stage]
        a = we_all.at[(i,) + tuple(slice(None) if d in done else pos[d] for d in (d3, d2, d1))]
        done = WR_PATHS[i][:stage]
        b = wr_s.at[(i,) + tuple(slice(None) if d in done else pos[d] for d in (d2, d1))]
        copies = []
        for step in (1, 3, 2):
            dev = at(WE_PATHS[i][stage], step)
            copies.append(remote(a, a, sem_s.at[i, step - 1, 0], sem_r.at[i, step - 1, 0], dev))
            dev = at(WR_PATHS[i][stage], step)
            copies.append(remote(b, b, sem_s.at[i, step - 1, 1], sem_r.at[i, step - 1, 1], dev))
        return copies

    def we_block(i, p, half=None):
        index, cut = [i], half is None
        for d in ORDERS[i][::-1]:
            if d == WE_PATHS[i][2]:
                index.append(p)
            elif cut:
                index.append(slice(None))
            else:
                index.append(pl.ds(2 * half, 2))
                cut = True
        return we_all.at[tuple(index)]

    def block_copies(which, i):
        axis_a, axis_b = WE_PATHS[i][2], WR_PATHS[i][2]
        copies = []
        for q, source, step in ((0, 3, 1), (1, 1, 3)):
            if which == 0:
                a = we_block(i, pos[axis_a])
                b = wr_t.at[i, :, pl.ds(pl.multiple_of(pos[axis_b] * 256, 256), 256)]
            else:
                a = we_block(i, (pos[axis_a] + source) % 4, q)
                o = (pos[axis_b] + source) % 4 * 256
                b = wr_t.at[i, pl.ds(512 * q, 512), pl.ds(pl.multiple_of(o, 256), 256)]
            n = 2 * which + q
            copies.append(remote(a, a, g3s.at[i, n, 0], g3r.at[i, n, 0], at(axis_a, step)))
            copies.append(remote(b, b, g3s.at[i, n, 1], g3r.at[i, n, 1], at(axis_b, step)))
        return copies

    g1 = [gather_copies(0, i) for i in range(3)]
    g2 = [gather_copies(1, i) for i in range(3)]
    g3 = [block_copies(0, i) for i in range(3)]
    g4 = [block_copies(1, i) for i in range(3)]

    def start(copies):
        for c in copies:
            c.start()

    def arrive(copies):
        for c in copies:
            c.wait_recv()

    def loop(lo, hi, body, unroll=1):
        def step(i, _):
            body(i)
            return 0
        lax.fori_loop(lo, hi, step, 0, unroll=unroll)

    def turn(i):
        col = pl.ds(pl.multiple_of(pos[ORDERS[i][2]] * 256, 256), 256)
        def piece(n):
            c = pl.multiple_of(n * 256, 256)
            rows = wr_s[i, :, :, :, pl.ds(c, 256)].astype(f32).reshape(256, 256)
            wr_t[i, pl.ds(c, 256), col] = rows.T.astype(bf16)
        loop(0, 4, piece)

    def a1_refs(k, to):
        src = s_send.at[k, pl.ds(8 * to, 8)]
        dst = s_recv.at[k, :, pl.ds(pl.multiple_of(16 * seq, 16), 16), :]
        return src, dst

    def a1_copy(k, r):
        to = (seq + r) % 16
        src, dst = a1_refs(k, to)
        return remote(src, dst, a1s.at[k, r], a1r.at[k, r], (to, ten))

    def a1_own(k):
        src, dst = a1_refs(k, seq)
        return pltpu.make_async_copy(src, dst, own_sem.at[0, k])

    def a2_refs(k, to):
        src = m_send.at[k, :, pl.ds(pl.multiple_of(16 * to, 16), 16), :]
        dst = m_recv.at[k, pl.ds(8 * seq, 8)]
        return src, dst

    def a2_copy(k, r):
        to = (seq + r) % 16
        src, dst = a2_refs(k, to)
        return remote(src, dst, a2s.at[k, r], a2r.at[k, r], (to, ten))

    def a2_own(k):
        src, dst = a2_refs(k, seq)
        return pltpu.make_async_copy(src, dst, own_sem.at[1, k])

    def a3_refs(k, to):
        src = r_send.at[k, to]
        dst = r_recv.at[pl.ds(2 * k, 2), pl.ds(pl.multiple_of(128 * ten, 128), 128)]
        return src, dst

    def a3_copy(k, r):
        to = (ten + r) % 8
        src, dst = a3_refs(k, to)
        return remote(src, dst, a3s.at[k, r], a3r.at[k, r], (seq, to))

    def a3_own(k):
        src, dst = a3_refs(k, ten)
        return pltpu.make_async_copy(src, dst, own_sem.at[2, k])

    def a4_refs(b, to):
        src = o_send.at[b, pl.ds(pl.multiple_of(to * 128, 128), 128)]
        dst = out.at[:, pl.ds(pl.multiple_of(ten * 1024 + (b % 2) * 512 + (b // 2) * TB, TB), TB)]
        return src, dst

    def a4_copy(b, r):
        to = (ten + r) % 8
        src, dst = a4_refs(b, to)
        return remote(src, dst, a4s.at[b, r], a4r.at[b, r], (seq, to))

    def a4_own(b):
        src, dst = a4_refs(b, ten)
        return pltpu.make_async_copy(src, dst, a4s.at[b, 0])

    def first(k):
        def block(a):
            value = jnp.dot(
                act_v[:, pl.ds(pl.multiple_of(a * 512, 512), 512)], f1_v[:, W * k:W * (k + 1)],
                preferred_element_type=f32)
            value = value * spec_v[:, pl.ds(pl.multiple_of(a * 512 + W * k, W), W)]
            for g in range(W // LANES):
                x32[g, pl.ds(a, 128, stride=16), :] = value[:, g * LANES:(g + 1) * LANES]
        loop(0, 16, block, 4)

    def send_first(k):
        def cast(n):
            c = 8 * n
            for g in range(W // LANES):
                rows = x32[g, pl.ds(pl.multiple_of(c * 16, 128), 128), :]
                s_send[k, pl.ds(c, 8), :, g * LANES:(g + 1) * LANES] = rows.astype(bf16).reshape(8, 16, LANES)
        loop(0, 16, cast)
        a1_own(k).start()
        loop(1, 16, lambda r: a1_copy(k, r).start())

    pl.semaphore_wait(barrier, 23)
    for c in wins:
        c.wait()
    for i in range(3):
        start(g1[i])
    for c in ins:
        c.wait()
    first(0)
    sc_t[...] = jnp.broadcast_to(sc_v[pl.ds(ten, 1), :], (LANES, LANES)).T
    sh_t[...] = jnp.broadcast_to(sh_v[pl.ds(ten, 1), :], (LANES, LANES)).T
    f2_b[...] = f2_v[...].astype(bf16)

    send_first(0)
    first(1)
    for i in range(3):
        arrive(g1[i])
        start(g2[i])

    def mixing(k):
        a1_own(k).wait()
        loop(1, 16, lambda r: a1_copy(k, r).wait_recv())
        if k == 0:
            send_first(1)
        def mix(c):
            m_send[k, c] = jnp.dot(f2_b[...], s_recv[k, c], preferred_element_type=f32).astype(bf16)
        loop(0, 8, mix)
        a2_own(k).start()
        loop(1, 16, lambda r: a2_copy(k, r).start())

    mixing(0)
    arrive(g2[0])
    turn(0)
    start(g3[0])
    mixing(1)
    for i in (1, 2):
        arrive(g2[i])
        turn(i)
        start(g3[i])

    def gating(k):
        a2_own(k).wait()
        loop(1, 16, lambda r: a2_copy(k, r).wait_recv())
        def widen(n):
            c = 8 * n
            rows = m_recv[k, pl.ds(c, 8)].astype(f32).reshape(128, W)
            for g in range(W // LANES):
                x32[g, pl.ds(pl.multiple_of(c * 16, 128), 128), :] = rows[:, g * LANES:(g + 1) * LANES]
        loop(0, 16, widen)
        def gate(p):
            for g in range(W // LANES):
                mixed = x32[g, pl.ds(p, 128, stride=16), :]
                cols = pl.ds(pl.multiple_of(p * 512 + W * k + g * LANES, LANES), LANES)
                value = act_v[:, cols].astype(f32)
                sig = jax.nn.sigmoid(value * sc_t[...] + sh_t[...])
                r_send[k, p // 2, p % 2, :, g * LANES:(g + 1) * LANES] = (value + sig * mixed).astype(bf16)
        loop(0, 16, gate)
        a3_own(k).start()
        loop(1, 8, lambda r: a3_copy(k, r).start())

    gating(0)
    arrive(g3[0])
    start(g4[0])
    gating(1)

    def norm_copy(b):
        return remote(n_all.at[0, b], n_all.at[1, b], ns.at[b], nr.at[b], partner)

    def normalize(b):
        def square(n, total):
            v = r_recv[b, pl.ds(pl.multiple_of(n * 64, 64), 64), :].astype(f32)
            return total + jnp.sum((v * v).reshape(8, 8, TB), axis=0)
        total = lax.fori_loop(0, 16, square, jnp.zeros((8, TB), f32))
        factor = lax.rsqrt(jnp.sum(total, axis=0, keepdims=True) * (1.0 / 1024) + epsilon)
        def write(n):
            rows = pl.ds(pl.multiple_of(n * 64, 64), 64)
            n_all[0, b, rows, :] = (r_recv[b, rows, :].astype(f32) * factor).astype(bf16)
        loop(0, 16, write)
        norm_copy(b).start()

    def mlp(i, blocks):
        for q, (which, b) in enumerate(blocks):
            product = jnp.dot(we_all[i].reshape(1024, 1024), n_all[which, b], preferred_element_type=f32)
            h_buf[q] = jax.nn.gelu(product).astype(bf16)
        return [jnp.dot(wr_t[i], h_buf[q], preferred_element_type=f32) for q in range(2)]

    def part_copy(b):
        return remote(p_send.at[b], p_recv.at[b], ps.at[b], pr.at[b], partner)

    def opening(which, n):
        acc[which, 2 * n], acc[which, 2 * n + 1] = mlp(0, ((which, 2 * n), (which, 2 * n + 1)))

    def middle(b):
        part, total = mlp(1, ((1, b), (0, b)))
        acc[1, b] += part
        acc[0, b] += total

    def last(b):
        part, total = mlp(2, ((1, b), (0, b)))
        p_send[b] = (acc[1, b] + part).astype(bf16)
        part_copy(b).start()
        acc[0, b] += total

    def finish(b):
        part_copy(b).wait_recv()
        o_send[b] = (r_recv[b].astype(f32) + (acc[0, b] + p_recv[b].astype(f32))).astype(bf16)
        a4_own(b).start()
        loop(1, 8, lambda r: a4_copy(b, r).start())

    def settle(k):
        a3_own(k).wait()
        loop(1, 8, lambda r: a3_copy(k, r).wait_recv())
        loop(2 * k, 2 * k + 2, normalize)

    settle(0)
    arrive(g3[1])
    start(g4[1])
    arrive(g4[0])
    loop(0, 1, lambda n: opening(0, n))
    loop(0, 2, lambda b: norm_copy(b).wait_recv())
    loop(0, 1, lambda n: opening(1, n))
    arrive(g3[2])
    start(g4[2])
    settle(1)
    loop(1, 2, lambda n: opening(0, n))
    loop(2, 4, lambda b: norm_copy(b).wait_recv())
    loop(1, 2, lambda n: opening(1, n))
    arrive(g4[1])
    loop(0, 2, middle)
    arrive(g4[2])
    last(0)
    last(1)
    finish(0)
    def tail(b):
        middle(b)
        finish(b - 1)
        last(b)
    loop(2, NT, tail)
    finish(NT - 1)

    def drain(b):
        a4_own(b).wait()
        loop(1, 8, lambda r: a4_copy(b, r).wait_recv())
        loop(1, 8, lambda r: a4_copy(b, r).wait_send())
        norm_copy(b).wait_send()
        part_copy(b).wait_send()
    loop(0, NT, drain)
    for i in range(3):
        for c in g1[i] + g2[i] + g3[i] + g4[i]:
            c.wait_send()
    for k in range(NK):
        loop(1, 16, lambda r, k=k: a1_copy(k, r).wait_send())
        loop(1, 16, lambda r, k=k: a2_copy(k, r).wait_send())
        loop(1, 8, lambda r, k=k: a3_copy(k, r).wait_send())


def on_device(act, f1, spec, f2, scale, shift, we, wr):
    vmem, dma = pltpu.VMEM, pltpu.SemaphoreType.DMA
    scratch = [
        vmem((128, 8192), bf16), vmem((512, 512), bf16), vmem((128, 8192), f32), vmem((256, 256), f32),
        vmem((256, 256), bf16), vmem((8, 128), f32), vmem((8, 128), f32),
        vmem((128, 128), f32), vmem((128, 128), f32),
        vmem((3, 4, 4, 4, 16, 1024), bf16), vmem((3, 4, 4, 16, 1024), bf16), vmem((3, 1024, 1024), bf16),
        vmem((W // 128, 2048, 128), f32),
        vmem((NK, 128, 16, W), bf16), vmem((NK, 8, 256, W), bf16),
        vmem((NK, 8, 256, W), bf16), vmem((NK, 128, 16, W), bf16),
        vmem((NK, 8, 2, 128, W), bf16), vmem((NT, 1024, TB), bf16),
        vmem((2, NT, 1024, TB), bf16), vmem((2, NT, 1024, TB), f32), vmem((2, 1024, TB), bf16),
        vmem((NT, 1024, TB), bf16), vmem((NT, 1024, TB), bf16), vmem((NT, 1024, TB), bf16),
        dma((6,)), dma((3, 2)), dma((3, NK)),
        dma((NK, 16)), dma((NK, 16)), dma((NK, 16)), dma((NK, 16)),
        dma((NK, 8)), dma((NK, 8)), dma((NT, 8)), dma((NT, 8)),
        dma((NT,)), dma((NT,)), dma((NT,)), dma((NT,)),
        dma((3, 3, 2)), dma((3, 3, 2)), dma((3, 3, 2)), dma((3, 3, 2)), dma((3, 4, 2)), dma((3, 4, 2)),
    ]
    return pl.pallas_call(
        kernel,
        out_shape=jax.ShapeDtypeStruct((128, 8192), bf16),
        in_specs=[pl.BlockSpec(memory_space=pl.ANY)] * 8,
        out_specs=pl.BlockSpec(memory_space=pl.ANY),
        scratch_shapes=scratch,
        compiler_params=pltpu.CompilerParams(
            collective_id=0, has_side_effects=True, vmem_limit_bytes=67_043_328),
        name="mixer",
    )(act, f1, spec, f2, scale.reshape(8, 128), shift.reshape(8, 128), we.T, wr)


def solution(mesh):
    return jax.shard_map(
        on_device,
        mesh=mesh,
        in_specs=(
            P("tensor", "seq"),
            P(),
            P("tensor", "seq"),
            P(),
            P(),
            P(),
            P(None, ("seq", "tensor")),
            P(("seq", "tensor"), None),
        ),
        out_specs=P("tensor", "seq"),
        check_vma=False,
    )
```

```python
import functools

import jax
import jax.numpy as jnp
from jax import lax
from jax.experimental import pallas as pl
from jax.experimental.pallas import tpu as pltpu
from jax.sharding import PartitionSpec as P

MESH = pl.DeviceIdType.MESH
NK = 2
W = 512 // NK
TB = 256
NT = 4
LANES = 128
ORDERS = (("y", "z", "x"), ("y", "x", "z"), ("y", "z", "x"))
WE_PATHS = (("y", "z", "x"), ("y", "x", "z"), ("z", "x", "y"))
WR_PATHS = (("z", "y", "x"), ("y", "x", "z"), ("z", "y", "x"))
epsilon = 1e-06
f32, bf16 = jnp.float32, jnp.bfloat16


def kernel(
    act, f1, spec, f2, scale, shift, we, wr, out,
    act_v, f1_v, spec_v, f2_v, f2_b, sc_v, sh_v, sc_t, sh_t,
    we_all, wr_s, wr_t, x32, s_send, s_recv, m_send, m_recv, r_send, r_recv,
    n_all, acc, h_buf, p_send, p_recv, o_send,
    in_sem, w_sem, own_sem, a1s, a1r, a2s, a2r, a3s, a3r, a4s, a4r, ns, nr, ps, pr,
    g1s, g1r, g2s, g2r, g3s, g3r,
):
    seq = lax.axis_index("seq")
    ten = lax.axis_index("tensor")
    core = seq % 2
    z = (seq // 2) % 4
    y_lo = seq // 8
    x = ten // 2
    y = (ten % 2) * 2 + y_lo
    pos = {"x": x, "y": y, "z": z}

    def at(axis, step):
        p = dict(pos)
        p[axis] = (p[axis] + step) % 4
        return ((p["y"] % 2) * 8 + p["z"] * 2 + core, p["x"] * 2 + p["y"] // 2)

    partner = (seq + 1 - 2 * core, ten)

    def remote(src, dst, s, r, dev):
        return pltpu.make_async_remote_copy(
            src_ref=src, dst_ref=dst, send_sem=s, recv_sem=r, device_id=dev, device_id_type=MESH
        )

    ins = [
        pltpu.make_async_copy(a, b, in_sem.at[i])
        for i, (a, b) in enumerate(
            ((act, act_v), (f1, f1_v), (spec, spec_v), (f2, f2_v), (scale, sc_v), (shift, sh_v))
        )
    ]
    wins = []
    for i, (d1, d2, d3) in enumerate(ORDERS):
        wins.append(pltpu.make_async_copy(
            we.at[pl.ds(16 * i, 16)], we_all.at[i, pos[d3], pos[d2], pos[d1]], w_sem.at[i, 0]))
        wins.append(pltpu.make_async_copy(
            wr.at[pl.ds(16 * i, 16)], wr_s.at[i, pos[d2], pos[d1]], w_sem.at[i, 1]))
    for c in wins + ins:
        c.start()

    barrier = pltpu.get_barrier_semaphore()
    for r in range(1, 16):
        pl.semaphore_signal(barrier, inc=1, device_id=((seq + r) % 16, ten), device_id_type=MESH)
    for r in range(1, 8):
        pl.semaphore_signal(barrier, inc=1, device_id=(seq, (ten + r) % 8), device_id_type=MESH)
    diagonal = ((1 - y_lo) * 8 + z * 2 + core, x * 2 + 1 - ten % 2)
    pl.semaphore_signal(barrier, inc=1, device_id=diagonal, device_id_type=MESH)

    def gather_copies(stage, i):
        sem_s, sem_r = ((g1s, g1r), (g2s, g2r))[stage]
        d1, d2, d3 = ORDERS[i]
        done = WE_PATHS[i][:stage]
        a = we_all.at[(i,) + tuple(slice(None) if d in done else pos[d] for d in (d3, d2, d1))]
        done = WR_PATHS[i][:stage]
        b = wr_s.at[(i,) + tuple(slice(None) if d in done else pos[d] for d in (d2, d1))]
        copies = []
        for step in (1, 3, 2):
            dev = at(WE_PATHS[i][stage], step)
            copies.append(remote(a, a, sem_s.at[i, step - 1, 0], sem_r.at[i, step - 1, 0], dev))
            dev = at(WR_PATHS[i][stage], step)
            copies.append(remote(b, b, sem_s.at[i, step - 1, 1], sem_r.at[i, step - 1, 1], dev))
        return copies

    def we_block(i, p, half=None):
        index, cut = [i], half is None
        for d in ORDERS[i][::-1]:
            if d == WE_PATHS[i][2]:
                index.append(p)
            elif cut:
                index.append(slice(None))
            else:
                index.append(pl.ds(2 * half, 2))
                cut = True
        return we_all.at[tuple(index)]

    def block_copies(which, i):
        axis_a, axis_b = WE_PATHS[i][2], WR_PATHS[i][2]
        copies = []
        for q, source, step in ((0, 3, 1), (1, 1, 3)):
            if which == 0:
                a = we_block(i, pos[axis_a])
                b = wr_t.at[i, :, pl.ds(pl.multiple_of(pos[axis_b] * 256, 256), 256)]
            else:
                a = we_block(i, (pos[axis_a] + source) % 4, q)
                o = (pos[axis_b] + source) % 4 * 256
                b = wr_t.at[i, pl.ds(512 * q, 512), pl.ds(pl.multiple_of(o, 256), 256)]
            n = 2 * which + q
            copies.append(remote(a, a, g3s.at[i, n, 0], g3r.at[i, n, 0], at(axis_a, step)))
            copies.append(remote(b, b, g3s.at[i, n, 1], g3r.at[i, n, 1], at(axis_b, step)))
        return copies

    g1 = [gather_copies(0, i) for i in range(3)]
    g2 = [gather_copies(1, i) for i in range(3)]
    g3 = [block_copies(0, i) for i in range(3)]
    g4 = [block_copies(1, i) for i in range(3)]

    def start(copies):
        for c in copies:
            c.start()

    def arrive(copies):
        for c in copies:
            c.wait_recv()

    def loop(lo, hi, body, unroll=1):
        def step(i, _):
            body(i)
            return 0
        lax.fori_loop(lo, hi, step, 0, unroll=unroll)

    def turn(i):
        col = pl.ds(pl.multiple_of(pos[ORDERS[i][2]] * 256, 256), 256)
        def piece(n):
            c = pl.multiple_of(n * 256, 256)
            rows = wr_s[i, :, :, :, pl.ds(c, 256)].astype(f32).reshape(256, 256)
            wr_t[i, pl.ds(c, 256), col] = rows.T.astype(bf16)
        loop(0, 4, piece)

    def a1_refs(k, to):
        src = s_send.at[k, pl.ds(8 * to, 8)]
        dst = s_recv.at[k, :, pl.ds(pl.multiple_of(16 * seq, 16), 16), :]
        return src, dst

    def a1_copy(k, r):
        to = (seq + r) % 16
        src, dst = a1_refs(k, to)
        return remote(src, dst, a1s.at[k, r], a1r.at[k, r], (to, ten))

    def a1_own(k):
        src, dst = a1_refs(k, seq)
        return pltpu.make_async_copy(src, dst, own_sem.at[0, k])

    def a2_refs(k, to):
        src = m_send.at[k, :, pl.ds(pl.multiple_of(16 * to, 16), 16), :]
        dst = m_recv.at[k, pl.ds(8 * seq, 8)]
        return src, dst

    def a2_copy(k, r):
        to = (seq + r) % 16
        src, dst = a2_refs(k, to)
        return remote(src, dst, a2s.at[k, r], a2r.at[k, r], (to, ten))

    def a2_own(k):
        src, dst = a2_refs(k, seq)
        return pltpu.make_async_copy(src, dst, own_sem.at[1, k])

    def a3_refs(k, to):
        src = r_send.at[k, to]
        dst = r_recv.at[pl.ds(2 * k, 2), pl.ds(pl.multiple_of(128 * ten, 128), 128)]
        return src, dst

    def a3_copy(k, r):
        to = (ten + r) % 8
        src, dst = a3_refs(k, to)
        return remote(src, dst, a3s.at[k, r], a3r.at[k, r], (seq, to))

    def a3_own(k):
        src, dst = a3_refs(k, ten)
        return pltpu.make_async_copy(src, dst, own_sem.at[2, k])

    def a4_refs(b, to):
        src = o_send.at[b, pl.ds(pl.multiple_of(to * 128, 128), 128)]
        dst = out.at[:, pl.ds(pl.multiple_of(ten * 1024 + (b % 2) * 512 + (b // 2) * TB, TB), TB)]
        return src, dst

    def a4_copy(b, r):
        to = (ten + r) % 8
        src, dst = a4_refs(b, to)
        return remote(src, dst, a4s.at[b, r], a4r.at[b, r], (seq, to))

    def a4_own(b):
        src, dst = a4_refs(b, ten)
        return pltpu.make_async_copy(src, dst, a4s.at[b, 0])

    def first(k):
        def block(a):
            value = jnp.dot(
                act_v[:, pl.ds(pl.multiple_of(a * 512, 512), 512)], f1_v[:, W * k:W * (k + 1)],
                preferred_element_type=f32)
            value = value * spec_v[:, pl.ds(pl.multiple_of(a * 512 + W * k, W), W)]
            for g in range(W // LANES):
                x32[g, pl.ds(a, 128, stride=16), :] = value[:, g * LANES:(g + 1) * LANES]
        loop(0, 16, block, 4)

    def send_first(k):
        def cast(n):
            c = 8 * n
            for g in range(W // LANES):
                rows = x32[g, pl.ds(pl.multiple_of(c * 16, 128), 128), :]
                s_send[k, pl.ds(c, 8), :, g * LANES:(g + 1) * LANES] = rows.astype(bf16).reshape(8, 16, LANES)
        loop(0, 16, cast)

    def send(k):
        a1_own(k).start()
        loop(1, 16, lambda r: a1_copy(k, r).start())

    pl.semaphore_wait(barrier, 23)
    for c in wins:
        c.wait()
    for i in range(3):
        start(g1[i])
    for c in ins:
        c.wait()
    first(0)
    sc_t[...] = jnp.broadcast_to(sc_v[pl.ds(ten, 1), :], (LANES, LANES)).T
    sh_t[...] = jnp.broadcast_to(sh_v[pl.ds(ten, 1), :], (LANES, LANES)).T
    f2_b[...] = f2_v[...].astype(bf16)

    send_first(0)
    send(0)
    first(1)
    send_first(1)
    for i in range(3):
        arrive(g1[i])
        start(g2[i])

    def mixing(k):
        a1_own(k).wait()
        loop(1, 16, lambda r: a1_copy(k, r).wait_recv())
        def mix(c):
            m_send[k, c] = jnp.dot(f2_b[...], s_recv[k, c], preferred_element_type=f32).astype(bf16)
        loop(0, 8, mix)
        a2_own(k).start()
        loop(1, 16, lambda r: a2_copy(k, r).start())

    def gating(k):
        a2_own(k).wait()
        loop(1, 16, lambda r: a2_copy(k, r).wait_recv())
        def widen(n):
            c = 8 * n
            rows = m_recv[k, pl.ds(c, 8)].astype(f32).reshape(128, W)
            for g in range(W // LANES):
                x32[g, pl.ds(pl.multiple_of(c * 16, 128), 128), :] = rows[:, g * LANES:(g + 1) * LANES]
        loop(0, 16, widen)
        def gate(p):
            for g in range(W // LANES):
                mixed = x32[g, pl.ds(p, 128, stride=16), :]
                cols = pl.ds(pl.multiple_of(p * 512 + W * k + g * LANES, LANES), LANES)
                value = act_v[:, cols].astype(f32)
                sig = jax.nn.sigmoid(value * sc_t[...] + sh_t[...])
                r_send[k, p // 2, p % 2, :, g * LANES:(g + 1) * LANES] = (value + sig * mixed).astype(bf16)
        loop(0, 16, gate)
        a3_own(k).start()
        loop(1, 8, lambda r: a3_copy(k, r).start())

    mixing(0)
    arrive(g2[0])
    turn(0)
    start(g3[0])
    send(1)
    for i in (1, 2):
        arrive(g2[i])
        turn(i)
        start(g3[i])
    gating(0)
    mixing(1)
    arrive(g3[0])
    start(g4[0])

    def norm_copy(b):
        return remote(n_all.at[0, b], n_all.at[1, b], ns.at[b], nr.at[b], partner)

    def normalize(b):
        def square(n, total):
            v = r_recv[b, pl.ds(pl.multiple_of(n * 64, 64), 64), :].astype(f32)
            return total + jnp.sum((v * v).reshape(8, 8, TB), axis=0)
        total = lax.fori_loop(0, 16, square, jnp.zeros((8, TB), f32))
        factor = lax.rsqrt(jnp.sum(total, axis=0, keepdims=True) * (1.0 / 1024) + epsilon)
        def write(n):
            rows = pl.ds(pl.multiple_of(n * 64, 64), 64)
            n_all[0, b, rows, :] = (r_recv[b, rows, :].astype(f32) * factor).astype(bf16)
        loop(0, 16, write)
        norm_copy(b).start()

    def mlp(i, blocks):
        for q, (which, b) in enumerate(blocks):
            product = jnp.dot(we_all[i].reshape(1024, 1024), n_all[which, b], preferred_element_type=f32)
            h_buf[q] = jax.nn.gelu(product).astype(bf16)
        return [jnp.dot(wr_t[i], h_buf[q], preferred_element_type=f32) for q in range(2)]

    def part_copy(b):
        return remote(p_send.at[b], p_recv.at[b], ps.at[b], pr.at[b], partner)

    def opening(which, n):
        acc[which, 2 * n], acc[which, 2 * n + 1] = mlp(0, ((which, 2 * n), (which, 2 * n + 1)))

    def middle(b):
        part, total = mlp(1, ((1, b), (0, b)))
        acc[1, b] += part
        acc[0, b] += total

    def last(b):
        part, total = mlp(2, ((1, b), (0, b)))
        p_send[b] = (acc[1, b] + part).astype(bf16)
        part_copy(b).start()
        acc[0, b] += total

    def finish(b):
        part_copy(b).wait_recv()
        o_send[b] = (r_recv[b].astype(f32) + (acc[0, b] + p_recv[b].astype(f32))).astype(bf16)
        a4_own(b).start()
        loop(1, 8, lambda r: a4_copy(b, r).start())

    def settle(k):
        a3_own(k).wait()
        loop(1, 8, lambda r: a3_copy(k, r).wait_recv())
        loop(2 * k, 2 * k + 2, normalize)

    settle(0)
    for i in (1, 2):
        arrive(g3[i])
        start(g4[i])
    gating(1)
    arrive(g4[0])
    loop(0, 1, lambda n: opening(0, n))
    loop(0, 2, lambda b: norm_copy(b).wait_recv())
    loop(0, 1, lambda n: opening(1, n))
    arrive(g4[1])
    loop(0, 2, middle)
    arrive(g4[2])
    loop(0, 2, last)
    settle(1)
    loop(0, 2, finish)
    loop(1, 2, lambda n: opening(0, n))
    loop(2, 4, lambda b: norm_copy(b).wait_recv())
    loop(1, 2, lambda n: opening(1, n))
    def tail(b):
        middle(b)
        @pl.when(b > 2)
        def _():
            finish(b - 1)
        last(b)
    loop(2, NT, tail)
    finish(NT - 1)

    def drain(b):
        a4_own(b).wait()
        loop(1, 8, lambda r: a4_copy(b, r).wait_recv())
        loop(1, 8, lambda r: a4_copy(b, r).wait_send())
        norm_copy(b).wait_send()
        part_copy(b).wait_send()
    loop(0, NT, drain)
    for i in range(3):
        for c in g1[i] + g2[i] + g3[i] + g4[i]:
            c.wait_send()
    for k in range(NK):
        loop(1, 16, lambda r, k=k: a1_copy(k, r).wait_send())
        loop(1, 16, lambda r, k=k: a2_copy(k, r).wait_send())
        loop(1, 8, lambda r, k=k: a3_copy(k, r).wait_send())


def on_device(act, f1, spec, f2, scale, shift, we, wr):
    vmem, dma = pltpu.VMEM, pltpu.SemaphoreType.DMA
    scratch = [
        vmem((128, 8192), bf16), vmem((512, 512), bf16), vmem((128, 8192), f32), vmem((256, 256), f32),
        vmem((256, 256), bf16), vmem((8, 128), f32), vmem((8, 128), f32),
        vmem((128, 128), f32), vmem((128, 128), f32),
        vmem((3, 4, 4, 4, 16, 1024), bf16), vmem((3, 4, 4, 16, 1024), bf16), vmem((3, 1024, 1024), bf16),
        vmem((W // 128, 2048, 128), f32),
        vmem((NK, 128, 16, W), bf16), vmem((NK, 8, 256, W), bf16),
        vmem((NK, 8, 256, W), bf16), vmem((NK, 128, 16, W), bf16),
        vmem((NK, 8, 2, 128, W), bf16), vmem((NT, 1024, TB), bf16),
        vmem((2, NT, 1024, TB), bf16), vmem((2, NT, 1024, TB), f32), vmem((2, 1024, TB), bf16),
        vmem((NT, 1024, TB), bf16), vmem((NT, 1024, TB), bf16), vmem((NT, 1024, TB), bf16),
        dma((6,)), dma((3, 2)), dma((3, NK)),
        dma((NK, 16)), dma((NK, 16)), dma((NK, 16)), dma((NK, 16)),
        dma((NK, 8)), dma((NK, 8)), dma((NT, 8)), dma((NT, 8)),
        dma((NT,)), dma((NT,)), dma((NT,)), dma((NT,)),
        dma((3, 3, 2)), dma((3, 3, 2)), dma((3, 3, 2)), dma((3, 3, 2)), dma((3, 4, 2)), dma((3, 4, 2)),
    ]
    return pl.pallas_call(
        kernel,
        out_shape=jax.ShapeDtypeStruct((128, 8192), bf16),
        in_specs=[pl.BlockSpec(memory_space=pl.ANY)] * 8,
        out_specs=pl.BlockSpec(memory_space=pl.ANY),
        scratch_shapes=scratch,
        compiler_params=pltpu.CompilerParams(
            collective_id=0, has_side_effects=True, vmem_limit_bytes=67_043_328),
        name="mixer",
    )(act, f1, spec, f2, scale.reshape(8, 128), shift.reshape(8, 128), we.T, wr)


def solution(mesh):
    return jax.shard_map(
        on_device,
        mesh=mesh,
        in_specs=(
            P("tensor", "seq"),
            P(),
            P("tensor", "seq"),
            P(),
            P(),
            P(),
            P(None, ("seq", "tensor")),
            P(("seq", "tensor"), None),
        ),
        out_specs=P("tensor", "seq"),
        check_vma=False,
    )
```

```python
import functools

import jax
import jax.numpy as jnp
from jax import lax
from jax.experimental import pallas as pl
from jax.experimental.pallas import tpu as pltpu
from jax.sharding import PartitionSpec as P

MESH = pl.DeviceIdType.MESH
NK = 2
W = 512 // NK
TB = 256
NT = 4
LANES = 128
ORDERS = (("y", "z", "x"), ("y", "x", "z"), ("y", "z", "x"))
WE_PATHS = (("y", "z", "x"), ("y", "x", "z"), ("z", "x", "y"))
WR_PATHS = (("z", "y", "x"), ("y", "x", "z"), ("z", "y", "x"))
epsilon = 1e-06
f32, bf16 = jnp.float32, jnp.bfloat16


def kernel(
    act, f1, spec, f2, scale, shift, we, wr, out,
    act_v, f1_v, spec_v, f2_v, f2_b, sc_v, sh_v, sc_t, sh_t,
    we_all, wr_s, wr_t, x32, s_send, s_recv, m_send, m_recv, r_send, r_recv,
    n_all, acc, h_buf, p_send, p_recv, o_send,
    in_sem, w_sem, own_sem, a1s, a1r, a2s, a2r, a3s, a3r, a4s, a4r, ns, nr, ps, pr,
    g1s, g1r, g2s, g2r, g3s, g3r,
):
    seq = lax.axis_index("seq")
    ten = lax.axis_index("tensor")
    core = seq % 2
    z = (seq // 2) % 4
    y_lo = seq // 8
    x = ten // 2
    y = (ten % 2) * 2 + y_lo
    pos = {"x": x, "y": y, "z": z}

    def at(axis, step):
        p = dict(pos)
        p[axis] = (p[axis] + step) % 4
        return ((p["y"] % 2) * 8 + p["z"] * 2 + core, p["x"] * 2 + p["y"] // 2)

    partner = (seq + 1 - 2 * core, ten)

    def remote(src, dst, s, r, dev):
        return pltpu.make_async_remote_copy(
            src_ref=src, dst_ref=dst, send_sem=s, recv_sem=r, device_id=dev, device_id_type=MESH
        )

    ins = [
        pltpu.make_async_copy(a, b, in_sem.at[i])
        for i, (a, b) in enumerate(
            ((act, act_v), (f1, f1_v), (spec, spec_v), (f2, f2_v), (scale, sc_v), (shift, sh_v))
        )
    ]
    wins = []
    for i, (d1, d2, d3) in enumerate(ORDERS):
        wins.append(pltpu.make_async_copy(
            we.at[pl.ds(16 * i, 16)], we_all.at[i, pos[d3], pos[d2], pos[d1]], w_sem.at[i, 0]))
        wins.append(pltpu.make_async_copy(
            wr.at[pl.ds(16 * i, 16)], wr_s.at[i, pos[d2], pos[d1]], w_sem.at[i, 1]))
    for c in wins + ins:
        c.start()

    barrier = pltpu.get_barrier_semaphore()
    for r in range(1, 16):
        pl.semaphore_signal(barrier, inc=1, device_id=((seq + r) % 16, ten), device_id_type=MESH)
    for r in range(1, 8):
        pl.semaphore_signal(barrier, inc=1, device_id=(seq, (ten + r) % 8), device_id_type=MESH)
    diagonal = ((1 - y_lo) * 8 + z * 2 + core, x * 2 + 1 - ten % 2)
    pl.semaphore_signal(barrier, inc=1, device_id=diagonal, device_id_type=MESH)

    def gather_copies(stage, i):
        sem_s, sem_r = ((g1s, g1r), (g2s, g2r))[stage]
        d1, d2, d3 = ORDERS[i]
        done = WE_PATHS[i][:stage]
        a = we_all.at[(i,) + tuple(slice(None) if d in done else pos[d] for d in (d3, d2, d1))]
        done = WR_PATHS[i][:stage]
        b = wr_s.at[(i,) + tuple(slice(None) if d in done else pos[d] for d in (d2, d1))]
        copies = []
        for step in (1, 3, 2):
            dev = at(WE_PATHS[i][stage], step)
            copies.append(remote(a, a, sem_s.at[i, step - 1, 0], sem_r.at[i, step - 1, 0], dev))
            dev = at(WR_PATHS[i][stage], step)
            copies.append(remote(b, b, sem_s.at[i, step - 1, 1], sem_r.at[i, step - 1, 1], dev))
        return copies

    def we_block(i, p, half=None):
        index, cut = [i], half is None
        for d in ORDERS[i][::-1]:
            if d == WE_PATHS[i][2]:
                index.append(p)
            elif cut:
                index.append(slice(None))
            else:
                index.append(pl.ds(2 * half, 2))
                cut = True
        return we_all.at[tuple(index)]

    def block_copies(which, i):
        axis_a, axis_b = WE_PATHS[i][2], WR_PATHS[i][2]
        copies = []
        for q, source, step in ((0, 3, 1), (1, 1, 3)):
            if which == 0:
                a = we_block(i, pos[axis_a])
                b = wr_t.at[i, :, pl.ds(pl.multiple_of(pos[axis_b] * 256, 256), 256)]
            else:
                a = we_block(i, (pos[axis_a] + source) % 4, q)
                o = (pos[axis_b] + source) % 4 * 256
                b = wr_t.at[i, pl.ds(512 * q, 512), pl.ds(pl.multiple_of(o, 256), 256)]
            n = 2 * which + q
            copies.append(remote(a, a, g3s.at[i, n, 0], g3r.at[i, n, 0], at(axis_a, step)))
            copies.append(remote(b, b, g3s.at[i, n, 1], g3r.at[i, n, 1], at(axis_b, step)))
        return copies

    g1 = [gather_copies(0, i) for i in range(3)]
    g2 = [gather_copies(1, i) for i in range(3)]
    g3 = [block_copies(0, i) for i in range(3)]
    g4 = [block_copies(1, i) for i in range(3)]

    def start(copies):
        for c in copies:
            c.start()

    def arrive(copies):
        for c in copies:
            c.wait_recv()

    def loop(lo, hi, body, unroll=1):
        def step(i, _):
            body(i)
            return 0
        lax.fori_loop(lo, hi, step, 0, unroll=unroll)

    def turn(i):
        col = pl.ds(pl.multiple_of(pos[ORDERS[i][2]] * 256, 256), 256)
        def piece(n):
            c = pl.multiple_of(n * 256, 256)
            rows = wr_s[i, :, :, :, pl.ds(c, 256)].astype(f32).reshape(256, 256)
            wr_t[i, pl.ds(c, 256), col] = rows.T.astype(bf16)
        loop(0, 4, piece)

    def a1_refs(k, to):
        src = s_send.at[k, pl.ds(8 * to, 8)]
        dst = s_recv.at[k, :, pl.ds(pl.multiple_of(16 * seq, 16), 16), :]
        return src, dst

    def a1_copy(k, r):
        to = (seq + r) % 16
        src, dst = a1_refs(k, to)
        return remote(src, dst, a1s.at[k, r], a1r.at[k, r], (to, ten))

    def a1_own(k):
        src, dst = a1_refs(k, seq)
        return pltpu.make_async_copy(src, dst, own_sem.at[0, k])

    def a2_refs(k, to):
        src = m_send.at[k, :, pl.ds(pl.multiple_of(16 * to, 16), 16), :]
        dst = m_recv.at[k, pl.ds(8 * seq, 8)]
        return src, dst

    def a2_copy(k, r):
        to = (seq + r) % 16
        src, dst = a2_refs(k, to)
        return remote(src, dst, a2s.at[k, r], a2r.at[k, r], (to, ten))

    def a2_own(k):
        src, dst = a2_refs(k, seq)
        return pltpu.make_async_copy(src, dst, own_sem.at[1, k])

    def a3_refs(k, to):
        src = r_send.at[k, to]
        dst = r_recv.at[pl.ds(2 * k, 2), pl.ds(pl.multiple_of(128 * ten, 128), 128)]
        return src, dst

    def a3_copy(k, r):
        to = (ten + r) % 8
        src, dst = a3_refs(k, to)
        return remote(src, dst, a3s.at[k, r], a3r.at[k, r], (seq, to))

    def a3_own(k):
        src, dst = a3_refs(k, ten)
        return pltpu.make_async_copy(src, dst, own_sem.at[2, k])

    def a4_refs(b, to):
        src = o_send.at[b, pl.ds(pl.multiple_of(to * 128, 128), 128)]
        dst = out.at[:, pl.ds(pl.multiple_of(ten * 1024 + (b % 2) * 512 + (b // 2) * TB, TB), TB)]
        return src, dst

    def a4_copy(b, r):
        to = (ten + r) % 8
        src, dst = a4_refs(b, to)
        return remote(src, dst, a4s.at[b, r], a4r.at[b, r], (seq, to))

    def a4_own(b):
        src, dst = a4_refs(b, ten)
        return pltpu.make_async_copy(src, dst, a4s.at[b, 0])

    def first(k):
        def block(a):
            value = jnp.dot(
                act_v[:, pl.ds(pl.multiple_of(a * 512, 512), 512)], f1_v[:, W * k:W * (k + 1)],
                preferred_element_type=f32)
            value = value * spec_v[:, pl.ds(pl.multiple_of(a * 512 + W * k, W), W)]
            for g in range(W // LANES):
                x32[g, pl.ds(a, 128, stride=16), :] = value[:, g * LANES:(g + 1) * LANES]
        loop(0, 16, block, 4)

    def send_first(k):
        def cast(n):
            c = 8 * n
            for g in range(W // LANES):
                rows = x32[g, pl.ds(pl.multiple_of(c * 16, 128), 128), :]
                s_send[k, pl.ds(c, 8), :, g * LANES:(g + 1) * LANES] = rows.astype(bf16).reshape(8, 16, LANES)
        loop(0, 16, cast)

    def send(k):
        a1_own(k).start()
        loop(1, 16, lambda r: a1_copy(k, r).start())

    pl.semaphore_wait(barrier, 23)
    for c in wins:
        c.wait()
    for i in range(3):
        start(g1[i])
    for c in ins:
        c.wait()
    first(0)
    sc_t[...] = jnp.broadcast_to(sc_v[pl.ds(ten, 1), :], (LANES, LANES)).T
    sh_t[...] = jnp.broadcast_to(sh_v[pl.ds(ten, 1), :], (LANES, LANES)).T
    f2_b[...] = f2_v[...].astype(bf16)

    send_first(0)
    send(0)
    first(1)
    send_first(1)
    for i in range(3):
        arrive(g1[i])
        start(g2[i])

    def mixing(k):
        a1_own(k).wait()
        loop(1, 16, lambda r: a1_copy(k, r).wait_recv())
        def mix(c):
            m_send[k, c] = jnp.dot(f2_b[...], s_recv[k, c], preferred_element_type=f32).astype(bf16)
        loop(0, 8, mix)
        a2_own(k).start()
        loop(1, 16, lambda r: a2_copy(k, r).start())

    def gating(k):
        a2_own(k).wait()
        loop(1, 16, lambda r: a2_copy(k, r).wait_recv())
        def widen(n):
            c = 8 * n
            rows = m_recv[k, pl.ds(c, 8)].astype(f32).reshape(128, W)
            for g in range(W // LANES):
                x32[g, pl.ds(pl.multiple_of(c * 16, 128), 128), :] = rows[:, g * LANES:(g + 1) * LANES]
        loop(0, 16, widen)
        def gate(p):
            for g in range(W // LANES):
                mixed = x32[g, pl.ds(p, 128, stride=16), :]
                cols = pl.ds(pl.multiple_of(p * 512 + W * k + g * LANES, LANES), LANES)
                value = act_v[:, cols].astype(f32)
                sig = jax.nn.sigmoid(value * sc_t[...] + sh_t[...])
                r_send[k, p // 2, p % 2, :, g * LANES:(g + 1) * LANES] = (value + sig * mixed).astype(bf16)
        loop(0, 16, gate)
        a3_own(k).start()
        loop(1, 8, lambda r: a3_copy(k, r).start())

    mixing(0)
    arrive(g2[0])
    turn(0)
    start(g3[0])
    send(1)
    for i in (1, 2):
        arrive(g2[i])
        turn(i)
        start(g3[i])
    gating(0)
    mixing(1)
    arrive(g3[0])
    start(g4[0])

    def norm_copy(b):
        return remote(n_all.at[0, b], n_all.at[1, b], ns.at[b], nr.at[b], partner)

    def normalize(b):
        def square(n, total):
            v = r_recv[b, pl.ds(pl.multiple_of(n * 64, 64), 64), :].astype(f32)
            return total + jnp.sum((v * v).reshape(8, 8, TB), axis=0)
        total = lax.fori_loop(0, 16, square, jnp.zeros((8, TB), f32))
        factor = lax.rsqrt(jnp.sum(total, axis=0, keepdims=True) * (1.0 / 1024) + epsilon)
        def write(n):
            rows = pl.ds(pl.multiple_of(n * 64, 64), 64)
            n_all[0, b, rows, :] = (r_recv[b, rows, :].astype(f32) * factor).astype(bf16)
        loop(0, 16, write)
        norm_copy(b).start()

    def mlp(i, blocks):
        for q, (which, b) in enumerate(blocks):
            product = jnp.dot(we_all[i].reshape(1024, 1024), n_all[which, b], preferred_element_type=f32)
            h_buf[q] = jax.nn.gelu(product).astype(bf16)
        return [jnp.dot(wr_t[i], h_buf[q], preferred_element_type=f32) for q in range(2)]

    def part_copy(b):
        return remote(p_send.at[b], p_recv.at[b], ps.at[b], pr.at[b], partner)

    def opening(which, n):
        acc[which, 2 * n], acc[which, 2 * n + 1] = mlp(0, ((which, 2 * n), (which, 2 * n + 1)))

    def middle(b):
        part, total = mlp(1, ((1, b), (0, b)))
        acc[1, b] += part
        acc[0, b] += total

    def last(b):
        part, total = mlp(2, ((1, b), (0, b)))
        p_send[b] = (acc[1, b] + part).astype(bf16)
        part_copy(b).start()
        acc[0, b] += total

    def finish(b):
        part_copy(b).wait_recv()
        o_send[b] = (r_recv[b].astype(f32) + (acc[0, b] + p_recv[b].astype(f32))).astype(bf16)
        a4_own(b).start()
        loop(1, 8, lambda r: a4_copy(b, r).start())

    def settle(k):
        a3_own(k).wait()
        loop(1, 8, lambda r: a3_copy(k, r).wait_recv())
        loop(2 * k, 2 * k + 2, normalize)

    arrive(g3[1])
    start(g4[1])
    settle(0)
    arrive(g3[2])
    start(g4[2])
    gating(1)
    arrive(g4[0])
    loop(0, 1, lambda n: opening(0, n))
    loop(0, 2, lambda b: norm_copy(b).wait_recv())
    loop(0, 1, lambda n: opening(1, n))
    arrive(g4[1])
    loop(0, 2, middle)
    arrive(g4[2])
    loop(0, 2, last)
    settle(1)
    loop(0, 2, finish)
    loop(1, 2, lambda n: opening(0, n))
    loop(2, 4, lambda b: norm_copy(b).wait_recv())
    loop(1, 2, lambda n: opening(1, n))
    def tail(b):
        middle(b)
        @pl.when(b > 2)
        def _():
            finish(b - 1)
        last(b)
    loop(2, NT, tail)
    finish(NT - 1)

    def drain(b):
        a4_own(b).wait()
        loop(1, 8, lambda r: a4_copy(b, r).wait_recv())
        loop(1, 8, lambda r: a4_copy(b, r).wait_send())
        norm_copy(b).wait_send()
        part_copy(b).wait_send()
    loop(0, NT, drain)
    for i in range(3):
        for c in g1[i] + g2[i] + g3[i] + g4[i]:
            c.wait_send()
    for k in range(NK):
        loop(1, 16, lambda r, k=k: a1_copy(k, r).wait_send())
        loop(1, 16, lambda r, k=k: a2_copy(k, r).wait_send())
        loop(1, 8, lambda r, k=k: a3_copy(k, r).wait_send())


def on_device(act, f1, spec, f2, scale, shift, we, wr):
    vmem, dma = pltpu.VMEM, pltpu.SemaphoreType.DMA
    scratch = [
        vmem((128, 8192), bf16), vmem((512, 512), bf16), vmem((128, 8192), f32), vmem((256, 256), f32),
        vmem((256, 256), bf16), vmem((8, 128), f32), vmem((8, 128), f32),
        vmem((128, 128), f32), vmem((128, 128), f32),
        vmem((3, 4, 4, 4, 16, 1024), bf16), vmem((3, 4, 4, 16, 1024), bf16), vmem((3, 1024, 1024), bf16),
        vmem((W // 128, 2048, 128), f32),
        vmem((NK, 128, 16, W), bf16), vmem((NK, 8, 256, W), bf16),
        vmem((NK, 8, 256, W), bf16), vmem((NK, 128, 16, W), bf16),
        vmem((NK, 8, 2, 128, W), bf16), vmem((NT, 1024, TB), bf16),
        vmem((2, NT, 1024, TB), bf16), vmem((2, NT, 1024, TB), f32), vmem((2, 1024, TB), bf16),
        vmem((NT, 1024, TB), bf16), vmem((NT, 1024, TB), bf16), vmem((NT, 1024, TB), bf16),
        dma((6,)), dma((3, 2)), dma((3, NK)),
        dma((NK, 16)), dma((NK, 16)), dma((NK, 16)), dma((NK, 16)),
        dma((NK, 8)), dma((NK, 8)), dma((NT, 8)), dma((NT, 8)),
        dma((NT,)), dma((NT,)), dma((NT,)), dma((NT,)),
        dma((3, 3, 2)), dma((3, 3, 2)), dma((3, 3, 2)), dma((3, 3, 2)), dma((3, 4, 2)), dma((3, 4, 2)),
    ]
    return pl.pallas_call(
        kernel,
        out_shape=jax.ShapeDtypeStruct((128, 8192), bf16),
        in_specs=[pl.BlockSpec(memory_space=pl.ANY)] * 8,
        out_specs=pl.BlockSpec(memory_space=pl.ANY),
        scratch_shapes=scratch,
        compiler_params=pltpu.CompilerParams(
            collective_id=0, has_side_effects=True, vmem_limit_bytes=67_043_328),
        name="mixer",
    )(act, f1, spec, f2, scale.reshape(8, 128), shift.reshape(8, 128), we.T, wr)


def solution(mesh):
    return jax.shard_map(
        on_device,
        mesh=mesh,
        in_specs=(
            P("tensor", "seq"),
            P(),
            P("tensor", "seq"),
            P(),
            P(),
            P(),
            P(None, ("seq", "tensor")),
            P(("seq", "tensor"), None),
        ),
        out_specs=P("tensor", "seq"),
        check_vma=False,
    )
```
